32 devices in a mesh: groups: 2 (over y), seq: 4 (over z), head: 4 (over x, core).
Axes of the slice: x: 2, y: 2, z: 4, core: 2. Of those that a mesh axis runs over, the one named last changes fastest.
Arguments:
- queries: bfloat16 [4096, 2048], P(('groups', 'seq'), 'head'), parts along dimension 0, may hold values from -8 to 8
- keys: bfloat16 [4096, 2048], P(('groups', 'seq'), 'head'), parts along dimension 0, may hold values from -8 to 8
- values: bfloat16 [4096, 2048], P(('groups', 'seq'), 'head'), parts along dimension 0, may hold values from -12 to 12
- w_out: bfloat16 [2048, 2048], replicated, may hold values from -0.125 to 0.125
Outputs:
- projected: bfloat16 [4096, 2048], P(('groups', 'seq', 'head')), parts along dimension 0
The draws below stay inside these ranges and needn't reach their ends.
There are 2 independent parts, one for each index of `groups`. The reference program is written for one: setup_inputs(seed, part) draws one part's arguments, and reference() takes and returns one part's arrays. A program takes and returns all parts, laid end to end along the dimension named above; an argument that names none is the same for every part. Nothing has to cross between parts.
All inputs are finite; a program needn't handle non-finite values.
Results may differ from the reference program's by a relative error of at most 0.005.
Values may be sent and summed in bfloat16 or wider, within the bound.
A program may use at most 128 MiB of HBM per device.

```python
import math
import jax
import jax.numpy as jnp
from jax import lax

HEADS = 16
HD = 128
D = 2048
WINDOW = 2048
TOKENS = 2048


def draw_queries(key, part):
    width = HEADS * HD
    spread = 1.4
    noise_key = jax.random.fold_in(key, 1)
    scale_key = jax.random.fold_in(key, 2)
    row_scale = jnp.exp(jax.random.uniform(scale_key, (TOKENS, 1), jnp.float32, math.log(0.7), math.log(2.0)))
    noise = jax.random.normal(noise_key, (TOKENS, width), jnp.float32)
    result = jnp.clip(noise * spread * row_scale, -8.0, 8.0)
    return result.astype(jnp.bfloat16)


def draw_keys(key, part):
    width = HEADS * HD
    spread = 1.6
    noise_key = jax.random.fold_in(key, 3)
    noise = jax.random.normal(noise_key, (TOKENS, width), jnp.float32)
    result = jnp.clip(noise * spread, -8.0, 8.0)
    return result.astype(jnp.bfloat16)


def draw_values(key, part):
    width = HEADS * HD
    noise_key = jax.random.fold_in(key, 5)
    column_scale = jnp.exp(jax.random.uniform(jax.random.fold_in(key, 6), (1, width), jnp.float32, math.log(0.3), math.log(3.0)))
    noise = jax.random.normal(noise_key, (TOKENS, width), jnp.float32)
    result = noise * column_scale
    return jnp.clip(result, -12.0, 12.0).astype(jnp.bfloat16)


def gaussian(rng, extent, scale, limit, kind=jnp.bfloat16):
    values = jax.random.normal(rng, extent, jnp.float32) * scale
    return jnp.minimum(jnp.maximum(values, -limit), limit).astype(kind)


def setup_inputs(seed: int = 0, part: int = 0) -> dict:
    arg_keys = jax.random.split(jax.random.key(seed), 5)
    part_splits = jax.random.split(jax.random.fold_in(arg_keys[4], part), 5)
    return {
        "queries": draw_queries(jax.random.fold_in(jax.random.fold_in(arg_keys[4], part), 71), part),
        "keys": draw_keys(jax.random.fold_in(jax.random.fold_in(arg_keys[4], part), 71), part),
        "values": draw_values(jax.random.fold_in(jax.random.fold_in(arg_keys[4], part), 71), part),
        "w_out": gaussian(arg_keys[3], (HEADS * HD, D), (HEADS * HD) ** -0.5, 0.125),
    }


def reference(queries, keys, values, w_out):
    block_rows = min(512, TOKENS)
    block_count = TOKENS // block_rows
    highest = lax.Precision.HIGHEST
    query_full = queries.astype(jnp.float32).reshape(TOKENS, HEADS, HD)
    key_full = keys.astype(jnp.float32).reshape(TOKENS, HEADS, HD)
    value_full = values.astype(jnp.float32).reshape(TOKENS, HEADS, HD)
    causal = jnp.arange(block_rows)[:, None] >= jnp.arange(block_rows)[None, :]

    def linear_step(state, inputs):
        query_part, key_part, value_part = inputs
        local = jnp.einsum('qhd,khd->hqk', query_part, key_part, precision=highest)
        local = jnp.where(causal[None], local, 0.0)
        intra = jnp.einsum('hqk,khe->qhe', local, value_part, precision=highest)
        inter = jnp.einsum('qhd,hde->qhe', query_part, state, precision=highest)
        state = state + jnp.einsum('khd,khe->hde', key_part, value_part, precision=highest)
        return (state, intra + inter)
    final_state, linear = lax.scan(linear_step, jnp.zeros((HEADS, HD, HD), jnp.float32), (query_full.reshape(block_count, block_rows, HEADS, HD), key_full.reshape(block_count, block_rows, HEADS, HD), value_full.reshape(block_count, block_rows, HEADS, HD)))
    linear = linear.reshape(TOKENS, HEADS, HD)
    normed = linear / jnp.sqrt(lax.optimization_barrier(jnp.mean(linear * linear, axis=-1, keepdims=True)) + 1e-06)
    span = WINDOW + block_rows
    wide_keys = jnp.concatenate([jnp.zeros((WINDOW, HEADS, HD), jnp.float32), key_full], 0)
    wide_values = jnp.concatenate([jnp.zeros((WINDOW, HEADS, HD), jnp.float32), value_full], 0)
    query_pos = jnp.arange(block_rows, dtype=jnp.int32)[:, None]
    key_pos = jnp.arange(span, dtype=jnp.int32)[None, :]
    band = (key_pos > query_pos) & (key_pos <= query_pos + WINDOW)
    scale = 1.0 / math.sqrt(HD)

    def window_block(index):
        begin = (index * block_rows).astype(jnp.int32)
        rows_q = lax.dynamic_slice_in_dim(query_full, begin, block_rows, 0)
        span_k = lax.dynamic_slice_in_dim(wide_keys, begin, span, 0)
        span_v = lax.dynamic_slice_in_dim(wide_values, begin, span, 0)
        valid = band & (begin - WINDOW + key_pos >= 0)
        scores = jnp.einsum('qhd,khd->hqk', rows_q, span_k, precision=highest) * scale
        scores = jnp.where(valid[None], scores, -1e+30)
        top = lax.optimization_barrier(jnp.max(scores, axis=-1, keepdims=True))
        expo = jnp.where(valid[None], jnp.exp(scores - top), 0.0)
        total = lax.optimization_barrier(jnp.sum(expo, axis=-1))
        weights = expo.astype(jnp.bfloat16).astype(jnp.float32)
        summed = jnp.einsum('hqk,khe->qhe', weights, span_v, precision=highest)
        return summed / jnp.transpose(total)[:, :, None]
    windowed = lax.map(window_block, jnp.arange(block_count, dtype=jnp.int32))
    windowed = windowed.reshape(TOKENS, HEADS, HD)
    mixed = (normed + windowed).astype(jnp.bfloat16).reshape(TOKENS, HEADS * HD)
    return jnp.dot(mixed, w_out, preferred_element_type=jnp.float32).astype(jnp.bfloat16)
```

```python
import functools
import math

import jax
import jax.numpy as jnp
from jax import lax
from jax.experimental import pallas as pl
from jax.experimental.pallas import tpu as pltpu
from jax.sharding import PartitionSpec as P

HD = 128
WINDOW = 2048
MESH = pl.DeviceIdType.MESH
F32 = jnp.float32
BF16 = jnp.bfloat16
RATE = math.log2(math.e) / math.sqrt(HD)
FLOOR = -1e30


def dot_nt(a, b):
    return lax.dot_general(a, b, (((1,), (1,)), ((), ())), preferred_element_type=F32)


def dot_tn(a, b):
    return lax.dot_general(a, b, (((0,), (0,)), ((), ())), preferred_element_type=F32)


def kernel(
    peers, q_ref, k_ref, v_ref, w_hbm, out_ref,
    w_ref, kbuf, vbuf, qbuf, o_send, o_recv, t_send, t_recv, s_send, s_recv, acc, lin, stat,
    mixed, gathered, w_sem, kv_tx, kv_rx, q_tx, q_rx, o_tx, o_rx, t_tx, t_rx, s_tx, s_rx, m_tx, m_rx,
):
    seq = lax.axis_index("seq")
    here = lax.axis_index("head")
    blocks = lax.axis_size("seq")
    length, width = q_ref.shape
    heads = width // HD
    share = length // peers

    load_w = pltpu.make_async_copy(w_hbm, w_ref, w_sem)
    load_w.start()

    barrier = pltpu.get_barrier_semaphore()
    for step in range(1, blocks):
        pl.semaphore_signal(
            barrier, inc=1, device_id={"seq": lax.rem(seq + step, blocks)}, device_id_type=MESH
        )
    for step in range(1, peers):
        pl.semaphore_signal(
            barrier, inc=1, device_id={"head": lax.rem(here + step, peers)}, device_id_type=MESH
        )
    pl.semaphore_wait(barrier, blocks - 1 + peers - 1)

    def cols(h):
        return pl.ds(pl.multiple_of(h * HD, HD), HD)

    def remote(source, target, tx, rx, device):
        return pltpu.make_async_remote_copy(
            src_ref=source, dst_ref=target, send_sem=tx, recv_sem=rx,
            device_id=device, device_id_type=MESH,
        )

    def key_copy(h):
        return remote(
            k_ref.at[:, cols(h)], kbuf.at[:, cols(h)], kv_tx.at[0, h], kv_rx.at[0, h], {"seq": 1}
        )

    def value_copy(h):
        return remote(
            v_ref.at[:, cols(h)], vbuf.at[:, cols(h)], kv_tx.at[1, h], kv_rx.at[1, h], {"seq": 1}
        )

    def query_copy(h, slot, target):
        return remote(
            q_ref.at[:, cols(h)], qbuf.at[slot, :, cols(h)],
            q_tx.at[slot, h], q_rx.at[slot, h], {"seq": target},
        )

    def relay_copy(h):
        return remote(
            qbuf.at[1, :, cols(h)], qbuf.at[1, :, cols(h)], q_tx.at[1, h], q_rx.at[1, h], {"seq": 1}
        )

    def part_copies(h, out_slot, in_slot, target):
        return (
            remote(
                t_send.at[out_slot, h], t_recv.at[in_slot, h],
                t_tx.at[out_slot, h], t_rx.at[in_slot, h], {"seq": target},
            ),
            remote(
                o_send.at[out_slot, h], o_recv.at[in_slot, h],
                o_tx.at[out_slot, h], o_rx.at[in_slot, h], {"seq": target},
            ),
        )

    def state_copy(h, tx_slot, in_slot, target):
        return remote(
            s_send.at[h], s_recv.at[in_slot, h], s_tx.at[tx_slot, h], s_rx.at[in_slot, h],
            {"seq": target},
        )

    def mixed_copy(h, step):
        target = lax.rem(here + step, peers)
        return remote(
            mixed.at[pl.ds(pl.multiple_of(h * HD, HD), HD), pl.ds(pl.multiple_of(target * share, HD), share)],
            gathered.at[pl.ds(pl.multiple_of(here * width + h * HD, HD), HD), :],
            m_tx.at[h, step], m_rx.at[h, step], {"head": target},
        )

    def loop(body):
        lax.fori_loop(0, heads, lambda h, c: (body(h), c)[1], 0)

    causal = lax.broadcasted_iota(jnp.int32, (length, length), 0) <= lax.broadcasted_iota(
        jnp.int32, (length, length), 1
    )

    def own(h):
        query, key, value = q_ref[:, cols(h)], k_ref[:, cols(h)], v_ref[:, cols(h)]
        scores = dot_nt(key, query)
        lin[h] = dot_tn(value, jnp.where(causal, scores, 0.0).astype(BF16))
        scores = jnp.where(causal, scores, FLOOR)
        top = jnp.max(scores, axis=0, keepdims=True)
        expo = jnp.exp2((scores - top) * RATE)
        stat[h, 0:1, :] = top
        stat[h, 1:2, :] = jnp.sum(expo, axis=0, keepdims=True)
        acc[h] = dot_tn(value, expo.astype(BF16))

    def part(query, pairs):
        scores = [dot_nt(key, query) for key, _ in pairs]
        top = functools.reduce(jnp.maximum, [jnp.max(s, axis=0, keepdims=True) for s in scores])
        expo = [jnp.exp2((s - top) * RATE) for s in scores]
        total = sum(jnp.sum(e, axis=0, keepdims=True) for e in expo)
        summed = sum(dot_tn(value, e.astype(BF16)) for e, (_, value) in zip(expo, pairs))
        return top, total, summed

    def emit(h, slot, top, total, summed):
        row = lax.broadcasted_iota(jnp.int32, t_send.shape[2:], 0)
        t_send[slot, h] = jnp.where(row == 0, top, total)
        o_send[slot, h] = (summed / total).astype(BF16)

    def merged(h, others):
        tops = [stat[h, 0:1, :]] + [o[0] for o in others]
        top = functools.reduce(jnp.maximum, tops)
        scale = jnp.exp2((tops[0] - top) * RATE)
        total = scale * stat[h, 1:2, :]
        summed = scale * acc[h]
        for other_top, other_total, other, normal in others:
            scale = jnp.exp2((other_top - top) * RATE)
            total += scale * other_total
            summed += (scale * other_total if normal else scale) * other
        return summed / total

    def received(h, slot):
        return t_recv[slot, h, 0:1, :], t_recv[slot, h, 1:2, :], o_recv[slot, h].astype(F32), True

    def finish(h, windowed, linear):
        square = jnp.mean(linear * linear, axis=0, keepdims=True)
        rows = pl.ds(pl.multiple_of(h * HD, HD), HD)
        mixed[rows, :] = (linear / jnp.sqrt(square + 1e-06) + windowed).astype(BF16)
        for step in range(1, peers):
            mixed_copy(h, step).start()
        gathered[pl.ds(pl.multiple_of(here * width + h * HD, HD), HD), :] = mixed[
            rows, pl.ds(pl.multiple_of(here * share, HD), share)
        ]

    @pl.when(seq == 0)
    def _():
        def send(h):
            key_copy(h).start()
            value_copy(h).start()

        def work(h):
            own(h)
            finish(h, acc[h] / stat[h, 1:2, :], lin[h])

        def drain(h):
            key_copy(h).wait_send()
            value_copy(h).wait_send()

        loop(send)
        loop(work)
        loop(drain)

    @pl.when(seq == 1)
    def _():
        def work(h):
            key_copy(h).wait_recv()
            value_copy(h).wait_recv()
            first = (kbuf[:, cols(h)], vbuf[:, cols(h)])
            second = (k_ref[:, cols(h)], v_ref[:, cols(h)])
            early = dot_tn(first[1], first[0])
            s_send[h] = (early + dot_tn(second[1], second[0])).astype(BF16)
            state_copy(h, 0, 0, 2).start()
            state_copy(h, 1, 0, 3).start()
            query_copy(h, 0, 1).wait_recv()
            emit(h, 0, *part(qbuf[0, :, cols(h)], (first, second)))
            for copy in part_copies(h, 0, 0, 2):
                copy.start()
            query = q_ref[:, cols(h)]
            windowed = merged(h, [part(query, (first,)) + (False,)])
            finish(h, windowed, lin[h] + dot_nt(early.astype(BF16), query))
            relay_copy(h).wait_recv()
            emit(h, 1, *part(qbuf[1, :, cols(h)], (first, second)))
            for copy in part_copies(h, 1, 0, 3):
                copy.start()

        def drain(h):
            state_copy(h, 0, 0, 2).wait_send()
            state_copy(h, 1, 0, 3).wait_send()
            for copy in part_copies(h, 0, 0, 2) + part_copies(h, 1, 0, 3):
                copy.wait_send()

        loop(own)
        loop(work)
        loop(drain)

    @pl.when(seq == 2)
    def _():
        def first(h):
            query_copy(h, 0, 1).start()
            own(h)
            key, value = k_ref[:, cols(h)], v_ref[:, cols(h)]
            s_send[h] = dot_tn(value, key).astype(BF16)
            state_copy(h, 0, 1, 3).start()
            query_copy(h, 1, 2).wait_recv()
            relay_copy(h).start()
            emit(h, 1, *part(qbuf[1, :, cols(h)], ((key, value),)))
            for copy in part_copies(h, 1, 1, 3):
                copy.start()

        def second(h):
            state_copy(h, 0, 0, 2).wait_recv()
            for copy in part_copies(h, 0, 0, 2):
                copy.wait_recv()
            linear = lin[h] + dot_nt(s_recv[0, h], q_ref[:, cols(h)])
            finish(h, merged(h, [received(h, 0)]), linear)

        def drain(h):
            query_copy(h, 0, 1).wait_send()
            relay_copy(h).wait_send()
            state_copy(h, 0, 1, 3).wait_send()
            for copy in part_copies(h, 1, 1, 3):
                copy.wait_send()

        loop(first)
        loop(second)
        loop(drain)

    @pl.when(seq == 3)
    def _():
        def send(h):
            query_copy(h, 1, 2).start()

        def work(h):
            state_copy(h, 0, 1, 3).wait_recv()
            state_copy(h, 1, 0, 3).wait_recv()
            for copy in part_copies(h, 1, 1, 3) + part_copies(h, 1, 0, 3):
                copy.wait_recv()
            query = q_ref[:, cols(h)]
            linear = lin[h] + dot_nt(s_recv[0, h], query) + dot_nt(s_recv[1, h], query)
            finish(h, merged(h, [received(h, 0), received(h, 1)]), linear)

        def drain(h):
            query_copy(h, 1, 2).wait_send()

        loop(send)
        loop(own)
        loop(work)
        loop(drain)

    load_w.wait()

    def collect(h):
        for step in range(1, peers):
            mixed_copy(h, step).wait()

    loop(collect)
    tile = math.gcd(w_ref.shape[1], 512)
    left = gathered[...].T

    @pl.loop(0, w_ref.shape[1] // tile)
    def _(index):
        part_cols = pl.ds(pl.multiple_of(index * tile, tile), tile)
        out_ref[:, part_cols] = jnp.dot(
            left, w_ref[:, part_cols], preferred_element_type=F32
        ).astype(BF16)


def fused(queries, keys, values, w_out):
    peers = lax.axis_size("head")
    length, width = queries.shape
    heads = width // HD
    share = length // peers
    dma = pltpu.SemaphoreType.DMA
    vmem = pl.BlockSpec(memory_space=pltpu.VMEM)
    return pl.pallas_call(
        functools.partial(kernel, peers),
        out_shape=jax.ShapeDtypeStruct((share, w_out.shape[1]), BF16),
        in_specs=[vmem, vmem, vmem, pl.BlockSpec(memory_space=pl.ANY)],
        out_specs=vmem,
        scratch_shapes=[
            pltpu.VMEM(w_out.shape, BF16),
            pltpu.VMEM((length, width), BF16),
            pltpu.VMEM((length, width), BF16),
            pltpu.VMEM((2, length, width), BF16),
            pltpu.VMEM((2, heads, HD, length), BF16),
            pltpu.VMEM((2, heads, HD, length), BF16),
            pltpu.VMEM((2, heads, 8, length), F32),
            pltpu.VMEM((2, heads, 8, length), F32),
            pltpu.VMEM((heads, HD, HD), BF16),
            pltpu.VMEM((2, heads, HD, HD), BF16),
            pltpu.VMEM((heads, HD, length), F32),
            pltpu.VMEM((heads, HD, length), F32),
            pltpu.VMEM((heads, 8, length), F32),
            pltpu.VMEM((width, length), BF16),
            pltpu.VMEM((peers * width, share), BF16),
            dma, dma((2, heads)), dma((2, heads)), dma((2, heads)), dma((2, heads)),
            dma((2, heads)), dma((2, heads)), dma((2, heads)), dma((2, heads)),
            dma((2, heads)), dma((2, heads)), dma((heads, peers)), dma((heads, peers)),
        ],
        compiler_params=pltpu.CompilerParams(
            collective_id=0, has_side_effects=True, vmem_limit_bytes=56 * 1024 * 1024
        ),
    )(queries, keys, values, w_out)


def shifted(value, axis, steps):
    count = lax.axis_size(axis)
    first, last = (max(0, -steps), min(count, count - steps))
    return lax.ppermute(value, axis, [(source, source + steps) for source in range(first, last)])


def fits(queries):
    length, width = queries.shape
    blocks = lax.axis_size("seq")
    share = length // lax.axis_size("head")
    return blocks == 4 and blocks * length <= WINDOW and share % HD == 0 and width % HD == 0


def per_device(queries, keys, values, w_out):
    if fits(queries):
        return fused(queries, keys, values, w_out)
    length_dev, width = queries.shape
    heads_dev = width // HD
    block_rows = min(512, length_dev)
    block_count = length_dev // block_rows
    highest = lax.Precision.HIGHEST
    seq_index = lax.axis_index("seq")
    q_blocks = queries.reshape(block_count, block_rows, heads_dev, HD)
    k_blocks = keys.reshape(block_count, block_rows, heads_dev, HD)
    v_blocks = values.reshape(block_count, block_rows, heads_dev, HD)
    block_states = jnp.einsum(
        "bkhd,bkhe->bhde", k_blocks, v_blocks, preferred_element_type=jnp.float32
    )
    own_state = jnp.sum(block_states, axis=0)
    earlier = jnp.cumsum(block_states, axis=0) - block_states
    piece = lax.all_gather(own_state[None], "seq", axis=0, tiled=True)
    order = jnp.arange(piece.shape[0], dtype=jnp.int32)
    keep = order < seq_index
    prefix = jnp.sum(jnp.where(keep[:, None, None, None], piece, 0.0), axis=0)
    causal = jnp.arange(block_rows)[:, None] >= jnp.arange(block_rows)[None, :]
    local_scores = jnp.einsum(
        "bqhd,bkhd->bhqk", q_blocks, k_blocks, preferred_element_type=jnp.float32
    )
    local_scores = jnp.where(causal, local_scores, 0.0)
    intra = jnp.einsum(
        "bhqk,bkhe->bqhe", local_scores, v_blocks.astype(jnp.float32), precision=highest
    )
    state_before = prefix[None] + earlier
    inter = jnp.einsum(
        "bqhd,bhde->bqhe", q_blocks.astype(jnp.float32), state_before, precision=highest
    )
    linear = (intra + inter).reshape(length_dev, heads_dev, HD)
    normed = linear / jnp.sqrt(jnp.mean(linear * linear, axis=-1, keepdims=True) + 1e-06)
    reach = min(WINDOW // length_dev, lax.axis_size("seq") - 1)
    received = [shifted((keys, values), "seq", distance) for distance in range(1, reach + 1)]
    pad_rows = WINDOW - reach * length_dev
    filler = jnp.zeros((pad_rows, width), keys.dtype)
    wide_keys = jnp.concatenate([filler] + [pair[0] for pair in reversed(received)] + [keys], 0)
    wide_values = jnp.concatenate([filler] + [pair[1] for pair in reversed(received)] + [values], 0)
    wide_keys = wide_keys.reshape(-1, heads_dev, HD)
    wide_values = wide_values.reshape(-1, heads_dev, HD)
    scale = 1.0 / math.sqrt(HD)
    span = WINDOW + block_rows
    query_pos = jnp.arange(block_rows, dtype=jnp.int32)[:, None]
    key_pos = jnp.arange(span, dtype=jnp.int32)[None, :]
    band = (key_pos > query_pos) & (key_pos <= query_pos + WINDOW)
    rows_q = queries.reshape(block_rows, heads_dev, HD)
    anchor = seq_index * length_dev + 0 - WINDOW
    valid = band & (anchor + key_pos >= 0)
    scores = (
        jnp.einsum("qhd,khd->hqk", rows_q, wide_keys, preferred_element_type=jnp.float32) * scale
    )
    scores = jnp.where(valid[None], scores, -1e30)
    top = jnp.max(scores, axis=-1, keepdims=True)
    expo = jnp.where(valid[None], jnp.exp(scores - top), 0.0)
    total = jnp.sum(expo, axis=-1)
    weights = expo.astype(jnp.bfloat16)
    summed = jnp.einsum("hqk,khe->qhe", weights, wide_values, preferred_element_type=jnp.float32)
    pieces = summed / jnp.transpose(total)[:, :, None]
    mixed = (normed + pieces).astype(jnp.bfloat16).reshape(length_dev, width)
    head_count = lax.axis_size("head")
    share = length_dev // head_count
    grouped = mixed.reshape(head_count, share, width)
    return jnp.dot(
        lax.all_to_all(grouped, "head", split_axis=0, concat_axis=2, tiled=True)[0],
        w_out,
        preferred_element_type=jnp.float32,
    ).astype(jnp.bfloat16)


def solution(mesh):
    return jax.shard_map(
        per_device,
        mesh=mesh,
        in_specs=(
            P(("groups", "seq"), "head"),
            P(("groups", "seq"), "head"),
            P(("groups", "seq"), "head"),
            P(),
        ),
        out_specs=P(("groups", "seq", "head"), None),
        check_vma=False,
    )
```

```python
import functools
import math

import jax
import jax.numpy as jnp
from jax import lax
from jax.experimental import pallas as pl
from jax.experimental.pallas import tpu as pltpu
from jax.sharding import PartitionSpec as P

HD = 128
WINDOW = 2048
MESH = pl.DeviceIdType.MESH
F32 = jnp.float32
BF16 = jnp.bfloat16
RATE = math.log2(math.e) / math.sqrt(HD)
FLOOR = -1e30


def dot_nt(a, b):
    return lax.dot_general(a, b, (((1,), (1,)), ((), ())), preferred_element_type=F32)


def dot_tn(a, b):
    return lax.dot_general(a, b, (((0,), (0,)), ((), ())), preferred_element_type=F32)


def kernel(
    peers, q_ref, k_ref, v_ref, w_hbm, out_ref,
    w_ref, summed, kbuf, vbuf, qbuf, o_send, o_recv, t_send, t_recv, s_send, s_recv, acc, lin, stat,
    mixed, gathered, w_sem, kv_tx, kv_rx, q_tx, q_rx, o_tx, o_rx, t_tx, t_rx, s_tx, s_rx, m_tx, m_rx,
):
    seq = lax.axis_index("seq")
    here = lax.axis_index("head")
    blocks = lax.axis_size("seq")
    length, width = q_ref.shape
    heads = width // HD
    share = length // peers

    def load_w(h, peer):
        return pltpu.make_async_copy(
            w_hbm.at[pl.ds(pl.multiple_of(peer * width + h * HD, HD), HD), :],
            w_ref.at[h, pl.ds(peer * HD, HD), :],
            w_sem.at[h, peer],
        )

    def load_head(h):
        for peer in range(peers):
            load_w(h, peer).start()

    lax.fori_loop(0, heads, lambda h, c: (load_head(h), c)[1], 0)

    barrier = pltpu.get_barrier_semaphore()
    for step in range(1, blocks):
        pl.semaphore_signal(
            barrier, inc=1, device_id={"seq": lax.rem(seq + step, blocks)}, device_id_type=MESH
        )
    for step in range(1, peers):
        pl.semaphore_signal(
            barrier, inc=1, device_id={"head": lax.rem(here + step, peers)}, device_id_type=MESH
        )
    pl.semaphore_wait(barrier, blocks - 1 + peers - 1)

    def cols(h):
        return pl.ds(pl.multiple_of(h * HD, HD), HD)

    def remote(source, target, tx, rx, device):
        return pltpu.make_async_remote_copy(
            src_ref=source, dst_ref=target, send_sem=tx, recv_sem=rx,
            device_id=device, device_id_type=MESH,
        )

    def key_copy(h):
        return remote(
            k_ref.at[:, cols(h)], kbuf.at[:, cols(h)], kv_tx.at[0, h], kv_rx.at[0, h], {"seq": 1}
        )

    def value_copy(h):
        return remote(
            v_ref.at[:, cols(h)], vbuf.at[:, cols(h)], kv_tx.at[1, h], kv_rx.at[1, h], {"seq": 1}
        )

    def query_copy(h, slot, target):
        return remote(
            q_ref.at[:, cols(h)], qbuf.at[slot, :, cols(h)],
            q_tx.at[slot, h], q_rx.at[slot, h], {"seq": target},
        )

    def relay_copy(h):
        return remote(
            qbuf.at[1, :, cols(h)], qbuf.at[1, :, cols(h)], q_tx.at[1, h], q_rx.at[1, h], {"seq": 1}
        )

    def part_copies(h, out_slot, in_slot, target):
        return (
            remote(
                t_send.at[out_slot, h], t_recv.at[in_slot, h],
                t_tx.at[out_slot, h], t_rx.at[in_slot, h], {"seq": target},
            ),
            remote(
                o_send.at[out_slot, h], o_recv.at[in_slot, h],
                o_tx.at[out_slot, h], o_rx.at[in_slot, h], {"seq": target},
            ),
        )

    def state_copy(h, tx_slot, in_slot, target):
        return remote(
            s_send.at[h], s_recv.at[in_slot, h], s_tx.at[tx_slot, h], s_rx.at[in_slot, h],
            {"seq": target},
        )

    def prefix_copy(h):
        return remote(
            s_recv.at[0, h], s_recv.at[0, h], s_tx.at[1, h], s_rx.at[0, h], {"seq": 3}
        )

    def mixed_copy(h, step):
        target = lax.rem(here + step, peers)
        return remote(
            mixed.at[pl.ds(pl.multiple_of(h * HD, HD), HD), pl.ds(pl.multiple_of(target * share, HD), share)],
            gathered.at[h, pl.ds(pl.multiple_of(here * HD, HD), HD), :],
            m_tx.at[h, step], m_rx.at[h, step], {"head": target},
        )

    def loop(body):
        lax.fori_loop(0, heads, lambda h, c: (body(h), c)[1], 0)

    causal = lax.broadcasted_iota(jnp.int32, (length, length), 0) <= lax.broadcasted_iota(
        jnp.int32, (length, length), 1
    )

    def own(h):
        query, key, value = q_ref[:, cols(h)], k_ref[:, cols(h)], v_ref[:, cols(h)]
        scores = dot_nt(key, query)
        kept = jnp.where(causal, scores, 0.0)
        coarse = kept.astype(BF16)
        fine = (kept - coarse.astype(F32)).astype(BF16)
        lin[h] = dot_tn(value, coarse) + dot_tn(value, fine)
        scores = jnp.where(causal, scores, FLOOR)
        top = jnp.max(scores, axis=0, keepdims=True)
        expo = jnp.exp2((scores - top) * RATE)
        stat[h, 0:1, :] = top
        stat[h, 1:2, :] = jnp.sum(expo, axis=0, keepdims=True)
        acc[h] = dot_tn(value, expo.astype(BF16))

    def part(query, pairs):
        scores = [dot_nt(key, query) for key, _ in pairs]
        top = functools.reduce(jnp.maximum, [jnp.max(s, axis=0, keepdims=True) for s in scores])
        expo = [jnp.exp2((s - top) * RATE) for s in scores]
        total = sum(jnp.sum(e, axis=0, keepdims=True) for e in expo)
        output = sum(dot_tn(value, e.astype(BF16)) for e, (_, value) in zip(expo, pairs))
        return top, total, output

    def emit(h, slot, top, total, output):
        row = lax.broadcasted_iota(jnp.int32, t_send.shape[2:], 0)
        t_send[slot, h] = jnp.where(row == 0, top, total)
        o_send[slot, h] = (output / total).astype(BF16)

    def merged(h, others):
        tops = [stat[h, 0:1, :]] + [o[0] for o in others]
        top = functools.reduce(jnp.maximum, tops)
        scale = jnp.exp2((tops[0] - top) * RATE)
        total = scale * stat[h, 1:2, :]
        output = scale * acc[h]
        for other_top, other_total, other, normal in others:
            scale = jnp.exp2((other_top - top) * RATE)
            total += scale * other_total
            output += (scale * other_total if normal else scale) * other
        return output / total

    def received(h, slot):
        return t_recv[slot, h, 0:1, :], t_recv[slot, h, 1:2, :], o_recv[slot, h].astype(F32), True

    def finish(h, windowed, linear):
        square = jnp.mean(linear * linear, axis=0, keepdims=True)
        rows = pl.ds(pl.multiple_of(h * HD, HD), HD)
        mixed[rows, :] = (linear / jnp.sqrt(square + 1e-06) + windowed).astype(BF16)
        for step in range(1, peers):
            mixed_copy(h, step).start()
        gathered[h, pl.ds(pl.multiple_of(here * HD, HD), HD), :] = mixed[
            rows, pl.ds(pl.multiple_of(here * share, HD), share)
        ]

    tile = math.gcd(w_ref.shape[2], 512)

    def project(h):
        for peer in range(peers):
            load_w(h, peer).wait()
        for step in range(1, peers):
            mixed_copy(h, step).wait()
        left = gathered[h].T

        @pl.loop(0, w_ref.shape[2] // tile)
        def _(index):
            part_cols = pl.ds(pl.multiple_of(index * tile, tile), tile)
            summed[:, part_cols] += jnp.dot(
                left, w_ref[h, :, part_cols], preferred_element_type=F32
            )

    def project_before(h):
        @pl.when(h > 0)
        def _():
            project(h - 1)

    summed[...] = jnp.zeros_like(summed)

    @pl.when(seq == 0)
    def _():
        def send(h):
            key_copy(h).start()
            value_copy(h).start()

        def work(h):
            own(h)
            finish(h, acc[h] / stat[h, 1:2, :], lin[h])
            project_before(h)

        def drain(h):
            key_copy(h).wait_send()
            value_copy(h).wait_send()

        loop(send)
        loop(work)
        loop(drain)

    @pl.when(seq == 1)
    def _():
        def work(h):
            project_before(h)
            key_copy(h).wait_recv()
            value_copy(h).wait_recv()
            first = (kbuf[:, cols(h)], vbuf[:, cols(h)])
            second = (k_ref[:, cols(h)], v_ref[:, cols(h)])
            early = dot_tn(first[1], first[0])
            s_send[h] = (early + dot_tn(second[1], second[0])).astype(BF16)
            state_copy(h, 0, 0, 2).start()
            query_copy(h, 0, 1).wait_recv()
            emit(h, 0, *part(qbuf[0, :, cols(h)], (first, second)))
            for copy in part_copies(h, 0, 0, 2):
                copy.start()
            query = q_ref[:, cols(h)]
            windowed = merged(h, [part(query, (first,)) + (False,)])
            finish(h, windowed, lin[h] + dot_nt(early.astype(BF16), query))
            relay_copy(h).wait_recv()
            emit(h, 1, *part(qbuf[1, :, cols(h)], (first, second)))
            for copy in part_copies(h, 1, 0, 3):
                copy.start()

        def drain(h):
            state_copy(h, 0, 0, 2).wait_send()
            for copy in part_copies(h, 0, 0, 2) + part_copies(h, 1, 0, 3):
                copy.wait_send()

        loop(own)
        loop(work)
        loop(drain)

    @pl.when(seq == 2)
    def _():
        def first(h):
            query_copy(h, 0, 1).start()
            own(h)
            key, value = k_ref[:, cols(h)], v_ref[:, cols(h)]
            s_send[h] = dot_tn(value, key).astype(BF16)
            state_copy(h, 0, 1, 3).start()
            query_copy(h, 1, 2).wait_recv()
            relay_copy(h).start()
            emit(h, 1, *part(qbuf[1, :, cols(h)], ((key, value),)))
            for copy in part_copies(h, 1, 1, 3):
                copy.start()

        def second(h):
            project_before(h)
            state_copy(h, 0, 0, 2).wait_recv()
            prefix_copy(h).start()
            for copy in part_copies(h, 0, 0, 2):
                copy.wait_recv()
            linear = lin[h] + dot_nt(s_recv[0, h], q_ref[:, cols(h)])
            finish(h, merged(h, [received(h, 0)]), linear)

        def drain(h):
            query_copy(h, 0, 1).wait_send()
            relay_copy(h).wait_send()
            state_copy(h, 0, 1, 3).wait_send()
            prefix_copy(h).wait_send()
            for copy in part_copies(h, 1, 1, 3):
                copy.wait_send()

        loop(first)
        loop(second)
        loop(drain)

    @pl.when(seq == 3)
    def _():
        def send(h):
            query_copy(h, 1, 2).start()

        def work(h):
            project_before(h)
            state_copy(h, 0, 1, 3).wait_recv()
            prefix_copy(h).wait_recv()
            for copy in part_copies(h, 1, 1, 3) + part_copies(h, 1, 0, 3):
                copy.wait_recv()
            query = q_ref[:, cols(h)]
            linear = lin[h] + dot_nt(s_recv[0, h], query) + dot_nt(s_recv[1, h], query)
            finish(h, merged(h, [received(h, 0), received(h, 1)]), linear)

        def drain(h):
            query_copy(h, 1, 2).wait_send()

        loop(send)
        loop(own)
        loop(work)
        loop(drain)

    project(heads - 1)
    out_ref[...] = summed[...].astype(BF16)


def fused(queries, keys, values, w_out):
    peers = lax.axis_size("head")
    length, width = queries.shape
    heads = width // HD
    share = length // peers
    dma = pltpu.SemaphoreType.DMA
    vmem = pl.BlockSpec(memory_space=pltpu.VMEM)
    return pl.pallas_call(
        functools.partial(kernel, peers),
        out_shape=jax.ShapeDtypeStruct((share, w_out.shape[1]), BF16),
        in_specs=[vmem, vmem, vmem, pl.BlockSpec(memory_space=pltpu.HBM)],
        out_specs=vmem,
        scratch_shapes=[
            pltpu.VMEM((heads, peers * HD, w_out.shape[1]), BF16),
            pltpu.VMEM((share, w_out.shape[1]), F32),
            pltpu.VMEM((length, width), BF16),
            pltpu.VMEM((length, width), BF16),
            pltpu.VMEM((2, length, width), BF16),
            pltpu.VMEM((2, heads, HD, length), BF16),
            pltpu.VMEM((2, heads, HD, length), BF16),
            pltpu.VMEM((2, heads, 2, length), F32),
            pltpu.VMEM((2, heads, 2, length), F32),
            pltpu.VMEM((heads, HD, HD), BF16),
            pltpu.VMEM((2, heads, HD, HD), BF16),
            pltpu.VMEM((heads, HD, length), F32),
            pltpu.VMEM((heads, HD, length), F32),
            pltpu.VMEM((heads, 8, length), F32),
            pltpu.VMEM((width, length), BF16),
            pltpu.VMEM((heads, peers * HD, share), BF16),
            dma((heads, peers)), dma((2, heads)), dma((2, heads)), dma((2, heads)), dma((2, heads)),
            dma((2, heads)), dma((2, heads)), dma((2, heads)), dma((2, heads)),
            dma((2, heads)), dma((2, heads)), dma((heads, peers)), dma((heads, peers)),
        ],
        compiler_params=pltpu.CompilerParams(
            collective_id=0, has_side_effects=True, vmem_limit_bytes=48 * 1024 * 1024
        ),
    )(queries, keys, values, w_out)


def shifted(value, axis, steps):
    count = lax.axis_size(axis)
    first, last = (max(0, -steps), min(count, count - steps))
    return lax.ppermute(value, axis, [(source, source + steps) for source in range(first, last)])


def fits(queries):
    length, width = queries.shape
    blocks = lax.axis_size("seq")
    share = length // lax.axis_size("head")
    return blocks == 4 and blocks * length <= WINDOW and share % HD == 0 and width % HD == 0


def per_device(queries, keys, values, w_out):
    if fits(queries):
        return fused(queries, keys, values, w_out)
    length_dev, width = queries.shape
    heads_dev = width // HD
    block_rows = min(512, length_dev)
    block_count = length_dev // block_rows
    highest = lax.Precision.HIGHEST
    seq_index = lax.axis_index("seq")
    q_blocks = queries.reshape(block_count, block_rows, heads_dev, HD)
    k_blocks = keys.reshape(block_count, block_rows, heads_dev, HD)
    v_blocks = values.reshape(block_count, block_rows, heads_dev, HD)
    block_states = jnp.einsum(
        "bkhd,bkhe->bhde", k_blocks, v_blocks, preferred_element_type=jnp.float32
    )
    own_state = jnp.sum(block_states, axis=0)
    earlier = jnp.cumsum(block_states, axis=0) - block_states
    piece = lax.all_gather(own_state[None], "seq", axis=0, tiled=True)
    order = jnp.arange(piece.shape[0], dtype=jnp.int32)
    keep = order < seq_index
    prefix = jnp.sum(jnp.where(keep[:, None, None, None], piece, 0.0), axis=0)
    causal = jnp.arange(block_rows)[:, None] >= jnp.arange(block_rows)[None, :]
    local_scores = jnp.einsum(
        "bqhd,bkhd->bhqk", q_blocks, k_blocks, preferred_element_type=jnp.float32
    )
    local_scores = jnp.where(causal, local_scores, 0.0)
    intra = jnp.einsum(
        "bhqk,bkhe->bqhe", local_scores, v_blocks.astype(jnp.float32), precision=highest
    )
    state_before = prefix[None] + earlier
    inter = jnp.einsum(
        "bqhd,bhde->bqhe", q_blocks.astype(jnp.float32), state_before, precision=highest
    )
    linear = (intra + inter).reshape(length_dev, heads_dev, HD)
    normed = linear / jnp.sqrt(jnp.mean(linear * linear, axis=-1, keepdims=True) + 1e-06)
    reach = min(WINDOW // length_dev, lax.axis_size("seq") - 1)
    received = [shifted((keys, values), "seq", distance) for distance in range(1, reach + 1)]
    pad_rows = WINDOW - reach * length_dev
    filler = jnp.zeros((pad_rows, width), keys.dtype)
    wide_keys = jnp.concatenate([filler] + [pair[0] for pair in reversed(received)] + [keys], 0)
    wide_values = jnp.concatenate([filler] + [pair[1] for pair in reversed(received)] + [values], 0)
    wide_keys = wide_keys.reshape(-1, heads_dev, HD)
    wide_values = wide_values.reshape(-1, heads_dev, HD)
    scale = 1.0 / math.sqrt(HD)
    span = WINDOW + block_rows
    query_pos = jnp.arange(block_rows, dtype=jnp.int32)[:, None]
    key_pos = jnp.arange(span, dtype=jnp.int32)[None, :]
    band = (key_pos > query_pos) & (key_pos <= query_pos + WINDOW)
    rows_q = queries.reshape(block_rows, heads_dev, HD)
    anchor = seq_index * length_dev + 0 - WINDOW
    valid = band & (anchor + key_pos >= 0)
    scores = (
        jnp.einsum("qhd,khd->hqk", rows_q, wide_keys, preferred_element_type=jnp.float32) * scale
    )
    scores = jnp.where(valid[None], scores, -1e30)
    top = jnp.max(scores, axis=-1, keepdims=True)
    expo = jnp.where(valid[None], jnp.exp(scores - top), 0.0)
    total = jnp.sum(expo, axis=-1)
    weights = expo.astype(jnp.bfloat16)
    summed = jnp.einsum("hqk,khe->qhe", weights, wide_values, preferred_element_type=jnp.float32)
    pieces = summed / jnp.transpose(total)[:, :, None]
    mixed = (normed + pieces).astype(jnp.bfloat16).reshape(length_dev, width)
    head_count = lax.axis_size("head")
    share = length_dev // head_count
    grouped = mixed.reshape(head_count, share, width)
    return jnp.dot(
        lax.all_to_all(grouped, "head", split_axis=0, concat_axis=2, tiled=True)[0],
        w_out,
        preferred_element_type=jnp.float32,
    ).astype(jnp.bfloat16)


def solution(mesh):
    return jax.shard_map(
        per_device,
        mesh=mesh,
        in_specs=(
            P(("groups", "seq"), "head"),
            P(("groups", "seq"), "head"),
            P(("groups", "seq"), "head"),
            P(),
        ),
        out_specs=P(("groups", "seq", "head"), None),
        check_vma=False,
    )
```

```python
import functools
import math

import jax
import jax.numpy as jnp
from jax import lax
from jax.experimental import pallas as pl
from jax.experimental.pallas import tpu as pltpu
from jax.sharding import PartitionSpec as P

HD = 128
WINDOW = 2048
MESH = pl.DeviceIdType.MESH
F32 = jnp.float32
BF16 = jnp.bfloat16
RATE = math.log2(math.e) / math.sqrt(HD)
FLOOR = -1e30


def dot_nt(a, b):
    return lax.dot_general(a, b, (((1,), (1,)), ((), ())), preferred_element_type=F32)


def dot_tn(a, b):
    return lax.dot_general(a, b, (((0,), (0,)), ((), ())), preferred_element_type=F32)


def kernel(
    peers, q_hbm, k_hbm, v_hbm, w_hbm, out_ref, q_ref, k_ref, v_ref,
    w_ref, summed, kbuf, vbuf, qbuf, o_send, o_recv, t_send, t_recv, s_send, s_recv, acc, lin, stat,
    mixed, gathered, in_sem, w_sem, kv_tx, kv_rx, q_tx, q_rx, o_tx, o_rx, t_tx, t_rx, s_tx, s_rx, m_tx, m_rx,
):
    seq = lax.axis_index("seq")
    here = lax.axis_index("head")
    blocks = lax.axis_size("seq")
    length, width = q_ref.shape
    heads = width // HD
    share = length // peers

    loads = [
        pltpu.make_async_copy(source, target, in_sem.at[i])
        for i, (source, target) in enumerate(((q_hbm, q_ref), (k_hbm, k_ref), (v_hbm, v_ref)))
    ]
    for load in loads:
        load.start()

    def load_w(h, peer):
        return pltpu.make_async_copy(
            w_hbm.at[pl.ds(pl.multiple_of(peer * width + h * HD, HD), HD), :],
            w_ref.at[h, pl.ds(peer * HD, HD), :],
            w_sem.at[h, peer],
        )

    def load_head(h):
        for peer in range(peers):
            load_w(h, peer).start()


    barrier = pltpu.get_barrier_semaphore()
    for step in range(1, blocks):
        pl.semaphore_signal(
            barrier, inc=1, device_id={"seq": lax.rem(seq + step, blocks)}, device_id_type=MESH
        )
    for step in range(1, peers):
        pl.semaphore_signal(
            barrier, inc=1, device_id={"head": lax.rem(here + step, peers)}, device_id_type=MESH
        )
    pl.semaphore_wait(barrier, blocks - 1 + peers - 1)
    for load in loads:
        load.wait()
    lax.fori_loop(0, heads, lambda h, c: (load_head(h), c)[1], 0)

    def cols(h):
        return pl.ds(pl.multiple_of(h * HD, HD), HD)

    def remote(source, target, tx, rx, device):
        return pltpu.make_async_remote_copy(
            src_ref=source, dst_ref=target, send_sem=tx, recv_sem=rx,
            device_id=device, device_id_type=MESH,
        )

    def key_copy(h):
        return remote(
            k_ref.at[:, cols(h)], kbuf.at[:, cols(h)], kv_tx.at[0, h], kv_rx.at[0, h], {"seq": 1}
        )

    def value_copy(h):
        return remote(
            v_ref.at[:, cols(h)], vbuf.at[:, cols(h)], kv_tx.at[1, h], kv_rx.at[1, h], {"seq": 1}
        )

    def query_copy(h, slot, target):
        return remote(
            q_ref.at[:, cols(h)], qbuf.at[slot, :, cols(h)],
            q_tx.at[slot, h], q_rx.at[slot, h], {"seq": target},
        )

    def relay_copy(h):
        return remote(
            qbuf.at[1, :, cols(h)], qbuf.at[1, :, cols(h)], q_tx.at[1, h], q_rx.at[1, h], {"seq": 1}
        )

    def part_copies(h, out_slot, in_slot, target):
        return (
            remote(
                t_send.at[out_slot, h], t_recv.at[in_slot, h],
                t_tx.at[out_slot, h], t_rx.at[in_slot, h], {"seq": target},
            ),
            remote(
                o_send.at[out_slot, h], o_recv.at[in_slot, h],
                o_tx.at[out_slot, h], o_rx.at[in_slot, h], {"seq": target},
            ),
        )

    def state_copy(h, tx_slot, in_slot, target):
        return remote(
            s_send.at[h], s_recv.at[in_slot, h], s_tx.at[tx_slot, h], s_rx.at[in_slot, h],
            {"seq": target},
        )

    def prefix_copy(h):
        return remote(
            s_recv.at[0, h], s_recv.at[0, h], s_tx.at[1, h], s_rx.at[0, h], {"seq": 3}
        )

    def mixed_copy(h, step):
        target = lax.rem(here + step, peers)
        return remote(
            mixed.at[pl.ds(pl.multiple_of(h * HD, HD), HD), pl.ds(pl.multiple_of(target * share, HD), share)],
            gathered.at[h, pl.ds(pl.multiple_of(here * HD, HD), HD), :],
            m_tx.at[h, step], m_rx.at[h, step], {"head": target},
        )

    def loop(body):
        lax.fori_loop(0, heads, lambda h, c: (body(h), c)[1], 0)

    causal = lax.broadcasted_iota(jnp.int32, (length, length), 0) <= lax.broadcasted_iota(
        jnp.int32, (length, length), 1
    )

    def own(h):
        query, key, value = q_ref[:, cols(h)], k_ref[:, cols(h)], v_ref[:, cols(h)]
        scores = dot_nt(key, query)
        kept = jnp.where(causal, scores, 0.0)
        coarse = kept.astype(BF16)
        fine = (kept - coarse.astype(F32)).astype(BF16)
        lin[h] = dot_tn(value, coarse) + dot_tn(value, fine)
        scores = jnp.where(causal, scores, FLOOR)
        top = jnp.max(scores, axis=0, keepdims=True)
        expo = jnp.exp2((scores - top) * RATE)
        stat[h, 0:1, :] = top
        stat[h, 1:2, :] = jnp.sum(expo, axis=0, keepdims=True)
        acc[h] = dot_tn(value, expo.astype(BF16))

    def part(query, pairs):
        scores = [dot_nt(key, query) for key, _ in pairs]
        top = functools.reduce(jnp.maximum, [jnp.max(s, axis=0, keepdims=True) for s in scores])
        expo = [jnp.exp2((s - top) * RATE) for s in scores]
        total = sum(jnp.sum(e, axis=0, keepdims=True) for e in expo)
        output = sum(dot_tn(value, e.astype(BF16)) for e, (_, value) in zip(expo, pairs))
        return top, total, output

    def emit(h, slot, top, total, output):
        row = lax.broadcasted_iota(jnp.int32, t_send.shape[2:], 0)
        t_send[slot, h] = jnp.where(row == 0, top, total)
        o_send[slot, h] = (output / total).astype(BF16)

    def merged(h, others):
        tops = [stat[h, 0:1, :]] + [o[0] for o in others]
        top = functools.reduce(jnp.maximum, tops)
        scale = jnp.exp2((tops[0] - top) * RATE)
        total = scale * stat[h, 1:2, :]
        output = scale * acc[h]
        for other_top, other_total, other, normal in others:
            scale = jnp.exp2((other_top - top) * RATE)
            total += scale * other_total
            output += (scale * other_total if normal else scale) * other
        return output / total

    def received(h, slot):
        return t_recv[slot, h, 0:1, :], t_recv[slot, h, 1:2, :], o_recv[slot, h].astype(F32), True

    def finish(h, windowed, linear):
        square = jnp.mean(linear * linear, axis=0, keepdims=True)
        rows = pl.ds(pl.multiple_of(h * HD, HD), HD)
        mixed[rows, :] = (linear / jnp.sqrt(square + 1e-06) + windowed).astype(BF16)
        for step in range(1, peers):
            mixed_copy(h, step).start()
        gathered[h, pl.ds(pl.multiple_of(here * HD, HD), HD), :] = mixed[
            rows, pl.ds(pl.multiple_of(here * share, HD), share)
        ]

    tile = math.gcd(w_ref.shape[2], 512)

    def project(h):
        for peer in range(peers):
            load_w(h, peer).wait()
        for step in range(1, peers):
            mixed_copy(h, step).wait()
        left = gathered[h].T

        @pl.loop(0, w_ref.shape[2] // tile)
        def _(index):
            part_cols = pl.ds(pl.multiple_of(index * tile, tile), tile)
            summed[:, part_cols] += jnp.dot(
                left, w_ref[h, :, part_cols], preferred_element_type=F32
            )

    def project_before(h):
        @pl.when(h > 0)
        def _():
            project(h - 1)

    summed[...] = jnp.zeros_like(summed)

    @pl.when(seq == 0)
    def _():
        def send(h):
            key_copy(h).start()
            value_copy(h).start()

        def work(h):
            own(h)
            finish(h, acc[h] / stat[h, 1:2, :], lin[h])
            project_before(h)

        def drain(h):
            key_copy(h).wait_send()
            value_copy(h).wait_send()

        loop(send)
        loop(work)
        loop(drain)

    @pl.when(seq == 1)
    def _():
        def work(h):
            project_before(h)
            key_copy(h).wait_recv()
            value_copy(h).wait_recv()
            first = (kbuf[:, cols(h)], vbuf[:, cols(h)])
            second = (k_ref[:, cols(h)], v_ref[:, cols(h)])
            early = dot_tn(first[1], first[0])
            s_send[h] = (early + dot_tn(second[1], second[0])).astype(BF16)
            state_copy(h, 0, 0, 2).start()
            relay_copy(h).wait_recv()
            emit(h, 1, *part(qbuf[1, :, cols(h)], (first, second)))
            for copy in part_copies(h, 1, 0, 3):
                copy.start()
            query_copy(h, 0, 1).wait_recv()
            emit(h, 0, *part(qbuf[0, :, cols(h)], (first, second)))
            for copy in part_copies(h, 0, 0, 2):
                copy.start()
            query = q_ref[:, cols(h)]
            windowed = merged(h, [part(query, (first,)) + (False,)])
            finish(h, windowed, lin[h] + dot_nt(early.astype(BF16), query))

        def drain(h):
            state_copy(h, 0, 0, 2).wait_send()
            for copy in part_copies(h, 0, 0, 2) + part_copies(h, 1, 0, 3):
                copy.wait_send()

        loop(own)
        loop(work)
        loop(drain)

    @pl.when(seq == 2)
    def _():
        def first(h):
            query_copy(h, 0, 1).start()
            own(h)
            key, value = k_ref[:, cols(h)], v_ref[:, cols(h)]
            s_send[h] = dot_tn(value, key).astype(BF16)
            state_copy(h, 0, 1, 3).start()
            query_copy(h, 1, 2).wait_recv()
            relay_copy(h).start()
            emit(h, 1, *part(qbuf[1, :, cols(h)], ((key, value),)))
            for copy in part_copies(h, 1, 1, 3):
                copy.start()

        def second(h):
            project_before(h)
            state_copy(h, 0, 0, 2).wait_recv()
            prefix_copy(h).start()
            for copy in part_copies(h, 0, 0, 2):
                copy.wait_recv()
            linear = lin[h] + dot_nt(s_recv[0, h], q_ref[:, cols(h)])
            finish(h, merged(h, [received(h, 0)]), linear)

        def drain(h):
            query_copy(h, 0, 1).wait_send()
            relay_copy(h).wait_send()
            state_copy(h, 0, 1, 3).wait_send()
            prefix_copy(h).wait_send()
            for copy in part_copies(h, 1, 1, 3):
                copy.wait_send()

        loop(first)
        loop(second)
        loop(drain)

    @pl.when(seq == 3)
    def _():
        def send(h):
            query_copy(h, 1, 2).start()

        def work(h):
            project_before(h)
            state_copy(h, 0, 1, 3).wait_recv()
            prefix_copy(h).wait_recv()
            for copy in part_copies(h, 1, 1, 3) + part_copies(h, 1, 0, 3):
                copy.wait_recv()
            query = q_ref[:, cols(h)]
            linear = lin[h] + dot_nt(s_recv[0, h], query) + dot_nt(s_recv[1, h], query)
            finish(h, merged(h, [received(h, 0), received(h, 1)]), linear)

        def drain(h):
            query_copy(h, 1, 2).wait_send()

        loop(send)
        loop(own)
        loop(work)
        loop(drain)

    project(heads - 1)
    out_ref[...] = summed[...].astype(BF16)


def fused(queries, keys, values, w_out):
    peers = lax.axis_size("head")
    length, width = queries.shape
    heads = width // HD
    share = length // peers
    dma = pltpu.SemaphoreType.DMA
    vmem = pl.BlockSpec(memory_space=pltpu.VMEM)
    return pl.pallas_call(
        functools.partial(kernel, peers),
        out_shape=jax.ShapeDtypeStruct((share, w_out.shape[1]), BF16),
        in_specs=[pl.BlockSpec(memory_space=pltpu.HBM)] * 4,
        out_specs=vmem,
        scratch_shapes=[
            pltpu.VMEM((length, width), BF16),
            pltpu.VMEM((length, width), BF16),
            pltpu.VMEM((length, width), BF16),
            pltpu.VMEM((heads, peers * HD, w_out.shape[1]), BF16),
            pltpu.VMEM((share, w_out.shape[1]), F32),
            pltpu.VMEM((length, width), BF16),
            pltpu.VMEM((length, width), BF16),
            pltpu.VMEM((2, length, width), BF16),
            pltpu.VMEM((2, heads, HD, length), BF16),
            pltpu.VMEM((2, heads, HD, length), BF16),
            pltpu.VMEM((2, heads, 2, length), F32),
            pltpu.VMEM((2, heads, 2, length), F32),
            pltpu.VMEM((heads, HD, HD), BF16),
            pltpu.VMEM((2, heads, HD, HD), BF16),
            pltpu.VMEM((heads, HD, length), F32),
            pltpu.VMEM((heads, HD, length), F32),
            pltpu.VMEM((heads, 8, length), F32),
            pltpu.VMEM((width, length), BF16),
            pltpu.VMEM((heads, peers * HD, share), BF16),
            dma((3,)), dma((heads, peers)), dma((2, heads)), dma((2, heads)), dma((2, heads)), dma((2, heads)),
            dma((2, heads)), dma((2, heads)), dma((2, heads)), dma((2, heads)),
            dma((2, heads)), dma((2, heads)), dma((heads, peers)), dma((heads, peers)),
        ],
        compiler_params=pltpu.CompilerParams(
            collective_id=0, has_side_effects=True, vmem_limit_bytes=48 * 1024 * 1024
        ),
    )(queries, keys, values, w_out)


def shifted(value, axis, steps):
    count = lax.axis_size(axis)
    first, last = (max(0, -steps), min(count, count - steps))
    return lax.ppermute(value, axis, [(source, source + steps) for source in range(first, last)])


def fits(queries):
    length, width = queries.shape
    blocks = lax.axis_size("seq")
    share = length // lax.axis_size("head")
    return blocks == 4 and blocks * length <= WINDOW and share % HD == 0 and width % HD == 0


def per_device(queries, keys, values, w_out):
    if fits(queries):
        return fused(queries, keys, values, w_out)
    length_dev, width = queries.shape
    heads_dev = width // HD
    block_rows = min(512, length_dev)
    block_count = length_dev // block_rows
    highest = lax.Precision.HIGHEST
    seq_index = lax.axis_index("seq")
    q_blocks = queries.reshape(block_count, block_rows, heads_dev, HD)
    k_blocks = keys.reshape(block_count, block_rows, heads_dev, HD)
    v_blocks = values.reshape(block_count, block_rows, heads_dev, HD)
    block_states = jnp.einsum(
        "bkhd,bkhe->bhde", k_blocks, v_blocks, preferred_element_type=jnp.float32
    )
    own_state = jnp.sum(block_states, axis=0)
    earlier = jnp.cumsum(block_states, axis=0) - block_states
    piece = lax.all_gather(own_state[None], "seq", axis=0, tiled=True)
    order = jnp.arange(piece.shape[0], dtype=jnp.int32)
    keep = order < seq_index
    prefix = jnp.sum(jnp.where(keep[:, None, None, None], piece, 0.0), axis=0)
    causal = jnp.arange(block_rows)[:, None] >= jnp.arange(block_rows)[None, :]
    local_scores = jnp.einsum(
        "bqhd,bkhd->bhqk", q_blocks, k_blocks, preferred_element_type=jnp.float32
    )
    local_scores = jnp.where(causal, local_scores, 0.0)
    intra = jnp.einsum(
        "bhqk,bkhe->bqhe", local_scores, v_blocks.astype(jnp.float32), precision=highest
    )
    state_before = prefix[None] + earlier
    inter = jnp.einsum(
        "bqhd,bhde->bqhe", q_blocks.astype(jnp.float32), state_before, precision=highest
    )
    linear = (intra + inter).reshape(length_dev, heads_dev, HD)
    normed = linear / jnp.sqrt(jnp.mean(linear * linear, axis=-1, keepdims=True) + 1e-06)
    reach = min(WINDOW // length_dev, lax.axis_size("seq") - 1)
    received = [shifted((keys, values), "seq", distance) for distance in range(1, reach + 1)]
    pad_rows = WINDOW - reach * length_dev
    filler = jnp.zeros((pad_rows, width), keys.dtype)
    wide_keys = jnp.concatenate([filler] + [pair[0] for pair in reversed(received)] + [keys], 0)
    wide_values = jnp.concatenate([filler] + [pair[1] for pair in reversed(received)] + [values], 0)
    wide_keys = wide_keys.reshape(-1, heads_dev, HD)
    wide_values = wide_values.reshape(-1, heads_dev, HD)
    scale = 1.0 / math.sqrt(HD)
    span = WINDOW + block_rows
    query_pos = jnp.arange(block_rows, dtype=jnp.int32)[:, None]
    key_pos = jnp.arange(span, dtype=jnp.int32)[None, :]
    band = (key_pos > query_pos) & (key_pos <= query_pos + WINDOW)
    rows_q = queries.reshape(block_rows, heads_dev, HD)
    anchor = seq_index * length_dev + 0 - WINDOW
    valid = band & (anchor + key_pos >= 0)
    scores = (
        jnp.einsum("qhd,khd->hqk", rows_q, wide_keys, preferred_element_type=jnp.float32) * scale
    )
    scores = jnp.where(valid[None], scores, -1e30)
    top = jnp.max(scores, axis=-1, keepdims=True)
    expo = jnp.where(valid[None], jnp.exp(scores - top), 0.0)
    total = jnp.sum(expo, axis=-1)
    weights = expo.astype(jnp.bfloat16)
    summed = jnp.einsum("hqk,khe->qhe", weights, wide_values, preferred_element_type=jnp.float32)
    pieces = summed / jnp.transpose(total)[:, :, None]
    mixed = (normed + pieces).astype(jnp.bfloat16).reshape(length_dev, width)
    head_count = lax.axis_size("head")
    share = length_dev // head_count
    grouped = mixed.reshape(head_count, share, width)
    return jnp.dot(
        lax.all_to_all(grouped, "head", split_axis=0, concat_axis=2, tiled=True)[0],
        w_out,
        preferred_element_type=jnp.float32,
    ).astype(jnp.bfloat16)


def solution(mesh):
    return jax.shard_map(
        per_device,
        mesh=mesh,
        in_specs=(
            P(("groups", "seq"), "head"),
            P(("groups", "seq"), "head"),
            P(("groups", "seq"), "head"),
            P(),
        ),
        out_specs=P(("groups", "seq", "head"), None),
        check_vma=False,
    )
```

```python
import functools
import math

import jax
import jax.numpy as jnp
from jax import lax
from jax.experimental import pallas as pl
from jax.experimental.pallas import tpu as pltpu
from jax.sharding import PartitionSpec as P

HD = 128
WINDOW = 2048
MESH = pl.DeviceIdType.MESH
F32 = jnp.float32
BF16 = jnp.bfloat16
RATE = math.log2(math.e) / math.sqrt(HD)
FLOOR = -1e30


def dot_nt(a, b):
    return lax.dot_general(a, b, (((1,), (1,)), ((), ())), preferred_element_type=F32)


def dot_tn(a, b):
    return lax.dot_general(a, b, (((0,), (0,)), ((), ())), preferred_element_type=F32)


def kernel(
    peers, q_hbm, k_hbm, v_hbm, w_hbm, out_ref, q_ref, k_ref, v_ref,
    w_ref, summed, kbuf, vbuf, qbuf, o_send, o_recv, t_send, t_recv, s_send, s_recv, acc, lin, stat,
    mixed, gathered, in_sem, w_sem, kv_tx, kv_rx, q_tx, q_rx, o_tx, o_rx, t_tx, t_rx, s_tx, s_rx, m_tx, m_rx,
):
    seq = lax.axis_index("seq")
    here = lax.axis_index("head")
    blocks = lax.axis_size("seq")
    length, width = q_ref.shape
    heads = width // HD
    share = length // peers

    loads = [
        pltpu.make_async_copy(source, target, in_sem.at[i])
        for i, (source, target) in enumerate(((q_hbm, q_ref), (k_hbm, k_ref), (v_hbm, v_ref)))
    ]
    for load in loads:
        load.start()

    def load_w(h, peer):
        return pltpu.make_async_copy(
            w_hbm.at[pl.ds(pl.multiple_of(peer * width + h * HD, HD), HD), :],
            w_ref.at[h, pl.ds(peer * HD, HD), :],
            w_sem.at[h, peer],
        )

    def load_head(h):
        for peer in range(peers):
            load_w(h, peer).start()


    barrier = pltpu.get_barrier_semaphore()
    for step in range(1, blocks):
        pl.semaphore_signal(
            barrier, inc=1, device_id={"seq": lax.rem(seq + step, blocks)}, device_id_type=MESH
        )
    for step in range(1, peers):
        pl.semaphore_signal(
            barrier, inc=1, device_id={"head": lax.rem(here + step, peers)}, device_id_type=MESH
        )
    pl.semaphore_wait(barrier, blocks - 1 + peers - 1)
    for load in loads:
        load.wait()
    lax.fori_loop(0, heads, lambda h, c: (load_head(h), c)[1], 0)

    def cols(h):
        return pl.ds(pl.multiple_of(h * HD, HD), HD)

    def remote(source, target, tx, rx, device):
        return pltpu.make_async_remote_copy(
            src_ref=source, dst_ref=target, send_sem=tx, recv_sem=rx,
            device_id=device, device_id_type=MESH,
        )

    def key_copy(h):
        return remote(
            k_ref.at[:, cols(h)], kbuf.at[:, cols(h)], kv_tx.at[0, h], kv_rx.at[0, h], {"seq": 1}
        )

    def value_copy(h):
        return remote(
            v_ref.at[:, cols(h)], vbuf.at[:, cols(h)], kv_tx.at[1, h], kv_rx.at[1, h], {"seq": 1}
        )

    def query_copy(h, slot, target):
        return remote(
            q_ref.at[:, cols(h)], qbuf.at[slot, :, cols(h)],
            q_tx.at[slot, h], q_rx.at[slot, h], {"seq": target},
        )

    def relay_copy(h):
        return remote(
            qbuf.at[1, :, cols(h)], qbuf.at[1, :, cols(h)], q_tx.at[1, h], q_rx.at[1, h], {"seq": 1}
        )

    def part_copies(h, out_slot, in_slot, target):
        return (
            remote(
                t_send.at[out_slot, h], t_recv.at[in_slot, h],
                t_tx.at[out_slot, h], t_rx.at[in_slot, h], {"seq": target},
            ),
            remote(
                o_send.at[out_slot, h], o_recv.at[in_slot, h],
                o_tx.at[out_slot, h], o_rx.at[in_slot, h], {"seq": target},
            ),
        )

    def state_copy(h, tx_slot, in_slot, target):
        return remote(
            s_send.at[h], s_recv.at[in_slot, h], s_tx.at[tx_slot, h], s_rx.at[in_slot, h],
            {"seq": target},
        )

    def prefix_copy(h):
        return remote(
            s_recv.at[0, h], s_recv.at[0, h], s_tx.at[1, h], s_rx.at[0, h], {"seq": 3}
        )

    def mixed_copy(h, step):
        target = lax.rem(here + step, peers)
        return remote(
            mixed.at[pl.ds(pl.multiple_of(h * HD, HD), HD), pl.ds(pl.multiple_of(target * share, HD), share)],
            gathered.at[h, pl.ds(pl.multiple_of(here * HD, HD), HD), :],
            m_tx.at[h, step], m_rx.at[h, step], {"head": target},
        )

    def loop(body):
        lax.fori_loop(0, heads, lambda h, c: (body(h), c)[1], 0)

    causal = lax.broadcasted_iota(jnp.int32, (length, length), 0) <= lax.broadcasted_iota(
        jnp.int32, (length, length), 1
    )

    def own(h):
        query, key, value = q_ref[:, cols(h)], k_ref[:, cols(h)], v_ref[:, cols(h)]
        scores = dot_nt(key, query)
        kept = jnp.where(causal, scores, 0.0)
        coarse = kept.astype(BF16)
        fine = (kept - coarse.astype(F32)).astype(BF16)
        lin[h] = dot_tn(value, coarse) + dot_tn(value, fine)
        scores = jnp.where(causal, scores, FLOOR)
        top = jnp.max(scores, axis=0, keepdims=True)
        expo = jnp.exp2((scores - top) * RATE)
        stat[h, 0:1, :] = top
        stat[h, 1:2, :] = jnp.sum(expo, axis=0, keepdims=True)
        acc[h] = dot_tn(value, expo.astype(BF16))

    def part(query, pairs):
        scores = [dot_nt(key, query) for key, _ in pairs]
        top = functools.reduce(jnp.maximum, [jnp.max(s, axis=0, keepdims=True) for s in scores])
        expo = [jnp.exp2((s - top) * RATE) for s in scores]
        total = sum(jnp.sum(e, axis=0, keepdims=True) for e in expo)
        output = sum(dot_tn(value, e.astype(BF16)) for e, (_, value) in zip(expo, pairs))
        return top, total, output

    def emit(h, slot, top, total, output):
        row = lax.broadcasted_iota(jnp.int32, t_send.shape[2:], 0)
        t_send[slot, h] = jnp.where(row == 0, top, total)
        o_send[slot, h] = (output / total).astype(BF16)

    def merged(h, others):
        tops = [stat[h, 0:1, :]] + [o[0] for o in others]
        top = functools.reduce(jnp.maximum, tops)
        scale = jnp.exp2((tops[0] - top) * RATE)
        total = scale * stat[h, 1:2, :]
        output = scale * acc[h]
        for other_top, other_total, other, normal in others:
            scale = jnp.exp2((other_top - top) * RATE)
            total += scale * other_total
            output += (scale * other_total if normal else scale) * other
        return output / total

    def received(h, slot):
        return t_recv[slot, h, 0:1, :], t_recv[slot, h, 1:2, :], o_recv[slot, h].astype(F32), True

    def finish(h, windowed, linear):
        square = jnp.mean(linear * linear, axis=0, keepdims=True)
        rows = pl.ds(pl.multiple_of(h * HD, HD), HD)
        mixed[rows, :] = (linear / jnp.sqrt(square + 1e-06) + windowed).astype(BF16)
        for step in range(1, peers):
            mixed_copy(h, step).start()
        gathered[h, pl.ds(pl.multiple_of(here * HD, HD), HD), :] = mixed[
            rows, pl.ds(pl.multiple_of(here * share, HD), share)
        ]

    tile = math.gcd(w_ref.shape[2], 512)

    def project(h):
        for peer in range(peers):
            load_w(h, peer).wait()
        for step in range(1, peers):
            mixed_copy(h, step).wait()
        left = gathered[h].T

        @pl.loop(0, w_ref.shape[2] // tile)
        def _(index):
            part_cols = pl.ds(pl.multiple_of(index * tile, tile), tile)
            summed[:, part_cols] += jnp.dot(
                left, w_ref[h, :, part_cols], preferred_element_type=F32
            )

    def project_before(h):
        @pl.when(h > 0)
        def _():
            project(h - 1)

    summed[...] = jnp.zeros_like(summed)

    @pl.when(seq == 0)
    def _():
        def send(h):
            key_copy(h).start()
            value_copy(h).start()

        def work(h):
            own(h)
            finish(h, acc[h] / stat[h, 1:2, :], lin[h])
            project_before(h)

        def drain(h):
            key_copy(h).wait_send()
            value_copy(h).wait_send()

        loop(send)
        loop(work)
        loop(drain)

    @pl.when(seq == 1)
    def _():
        def work(h):
            project_before(h)
            key_copy(h).wait_recv()
            value_copy(h).wait_recv()
            first = (kbuf[:, cols(h)], vbuf[:, cols(h)])
            second = (k_ref[:, cols(h)], v_ref[:, cols(h)])
            early = dot_tn(first[1], first[0])
            s_send[h] = (early + dot_tn(second[1], second[0])).astype(BF16)
            state_copy(h, 0, 0, 2).start()
            query_copy(h, 0, 1).wait_recv()
            emit(h, 0, *part(qbuf[0, :, cols(h)], (first, second)))
            for copy in part_copies(h, 0, 0, 2):
                copy.start()
            query = q_ref[:, cols(h)]
            windowed = merged(h, [part(query, (first,)) + (False,)])
            finish(h, windowed, lin[h] + dot_nt(early.astype(BF16), query))
            relay_copy(h).wait_recv()
            emit(h, 1, *part(qbuf[1, :, cols(h)], (first, second)))
            for copy in part_copies(h, 1, 0, 3):
                copy.start()

        def drain(h):
            state_copy(h, 0, 0, 2).wait_send()
            for copy in part_copies(h, 0, 0, 2) + part_copies(h, 1, 0, 3):
                copy.wait_send()

        loop(own)
        loop(work)
        loop(drain)

    @pl.when(seq == 2)
    def _():
        def first(h):
            query_copy(h, 0, 1).start()
            own(h)
            key, value = k_ref[:, cols(h)], v_ref[:, cols(h)]
            s_send[h] = dot_tn(value, key).astype(BF16)
            state_copy(h, 0, 1, 3).start()
            query_copy(h, 1, 2).wait_recv()
            relay_copy(h).start()
            emit(h, 1, *part(qbuf[1, :, cols(h)], ((key, value),)))
            for copy in part_copies(h, 1, 1, 3):
                copy.start()

        def second(h):
            project_before(h)
            state_copy(h, 0, 0, 2).wait_recv()
            prefix_copy(h).start()
            for copy in part_copies(h, 0, 0, 2):
                copy.wait_recv()
            linear = lin[h] + dot_nt(s_recv[0, h], q_ref[:, cols(h)])
            finish(h, merged(h, [received(h, 0)]), linear)

        def drain(h):
            query_copy(h, 0, 1).wait_send()
            relay_copy(h).wait_send()
            state_copy(h, 0, 1, 3).wait_send()
            prefix_copy(h).wait_send()
            for copy in part_copies(h, 1, 1, 3):
                copy.wait_send()

        loop(first)
        loop(second)
        loop(drain)

    @pl.when(seq == 3)
    def _():
        def send(h):
            query_copy(h, 1, 2).start()

        def work(h):
            project_before(h)
            state_copy(h, 0, 1, 3).wait_recv()
            prefix_copy(h).wait_recv()
            for copy in part_copies(h, 1, 1, 3) + part_copies(h, 1, 0, 3):
                copy.wait_recv()
            query = q_ref[:, cols(h)]
            linear = lin[h] + dot_nt(s_recv[0, h], query) + dot_nt(s_recv[1, h], query)
            finish(h, merged(h, [received(h, 0), received(h, 1)]), linear)

        def drain(h):
            query_copy(h, 1, 2).wait_send()

        loop(send)
        loop(own)
        loop(work)
        loop(drain)

    project(heads - 1)
    out_ref[...] = summed[...].astype(BF16)


def fused(queries, keys, values, w_out):
    peers = lax.axis_size("head")
    length, width = queries.shape
    heads = width // HD
    share = length // peers
    dma = pltpu.SemaphoreType.DMA
    vmem = pl.BlockSpec(memory_space=pltpu.VMEM)
    return pl.pallas_call(
        functools.partial(kernel, peers),
        out_shape=jax.ShapeDtypeStruct((share, w_out.shape[1]), BF16),
        in_specs=[pl.BlockSpec(memory_space=pltpu.HBM)] * 4,
        out_specs=vmem,
        scratch_shapes=[
            pltpu.VMEM((length, width), BF16),
            pltpu.VMEM((length, width), BF16),
            pltpu.VMEM((length, width), BF16),
            pltpu.VMEM((heads, peers * HD, w_out.shape[1]), BF16),
            pltpu.VMEM((share, w_out.shape[1]), F32),
            pltpu.VMEM((length, width), BF16),
            pltpu.VMEM((length, width), BF16),
            pltpu.VMEM((2, length, width), BF16),
            pltpu.VMEM((2, heads, HD, length), BF16),
            pltpu.VMEM((2, heads, HD, length), BF16),
            pltpu.VMEM((2, heads, 2, length), F32),
            pltpu.VMEM((2, heads, 2, length), F32),
            pltpu.VMEM((heads, HD, HD), BF16),
            pltpu.VMEM((2, heads, HD, HD), BF16),
            pltpu.VMEM((heads, HD, length), F32),
            pltpu.VMEM((heads, HD, length), F32),
            pltpu.VMEM((heads, 8, length), F32),
            pltpu.VMEM((width, length), BF16),
            pltpu.VMEM((heads, peers * HD, share), BF16),
            dma((3,)), dma((heads, peers)), dma((2, heads)), dma((2, heads)), dma((2, heads)), dma((2, heads)),
            dma((2, heads)), dma((2, heads)), dma((2, heads)), dma((2, heads)),
            dma((2, heads)), dma((2, heads)), dma((heads, peers)), dma((heads, peers)),
        ],
        compiler_params=pltpu.CompilerParams(
            collective_id=0, has_side_effects=True, vmem_limit_bytes=56 * 1024 * 1024
        ),
    )(queries, keys, values, w_out)


def shifted(value, axis, steps):
    count = lax.axis_size(axis)
    first, last = (max(0, -steps), min(count, count - steps))
    return lax.ppermute(value, axis, [(source, source + steps) for source in range(first, last)])


def fits(queries):
    length, width = queries.shape
    blocks = lax.axis_size("seq")
    share = length // lax.axis_size("head")
    return blocks == 4 and blocks * length <= WINDOW and share % HD == 0 and width % HD == 0


def per_device(queries, keys, values, w_out):
    if fits(queries):
        return fused(queries, keys, values, w_out)
    length_dev, width = queries.shape
    heads_dev = width // HD
    block_rows = min(512, length_dev)
    block_count = length_dev // block_rows
    highest = lax.Precision.HIGHEST
    seq_index = lax.axis_index("seq")
    q_blocks = queries.reshape(block_count, block_rows, heads_dev, HD)
    k_blocks = keys.reshape(block_count, block_rows, heads_dev, HD)
    v_blocks = values.reshape(block_count, block_rows, heads_dev, HD)
    block_states = jnp.einsum(
        "bkhd,bkhe->bhde", k_blocks, v_blocks, preferred_element_type=jnp.float32
    )
    own_state = jnp.sum(block_states, axis=0)
    earlier = jnp.cumsum(block_states, axis=0) - block_states
    piece = lax.all_gather(own_state[None], "seq", axis=0, tiled=True)
    order = jnp.arange(piece.shape[0], dtype=jnp.int32)
    keep = order < seq_index
    prefix = jnp.sum(jnp.where(keep[:, None, None, None], piece, 0.0), axis=0)
    causal = jnp.arange(block_rows)[:, None] >= jnp.arange(block_rows)[None, :]
    local_scores = jnp.einsum(
        "bqhd,bkhd->bhqk", q_blocks, k_blocks, preferred_element_type=jnp.float32
    )
    local_scores = jnp.where(causal, local_scores, 0.0)
    intra = jnp.einsum(
        "bhqk,bkhe->bqhe", local_scores, v_blocks.astype(jnp.float32), precision=highest
    )
    state_before = prefix[None] + earlier
    inter = jnp.einsum(
        "bqhd,bhde->bqhe", q_blocks.astype(jnp.float32), state_before, precision=highest
    )
    linear = (intra + inter).reshape(length_dev, heads_dev, HD)
    normed = linear / jnp.sqrt(jnp.mean(linear * linear, axis=-1, keepdims=True) + 1e-06)
    reach = min(WINDOW // length_dev, lax.axis_size("seq") - 1)
    received = [shifted((keys, values), "seq", distance) for distance in range(1, reach + 1)]
    pad_rows = WINDOW - reach * length_dev
    filler = jnp.zeros((pad_rows, width), keys.dtype)
    wide_keys = jnp.concatenate([filler] + [pair[0] for pair in reversed(received)] + [keys], 0)
    wide_values = jnp.concatenate([filler] + [pair[1] for pair in reversed(received)] + [values], 0)
    wide_keys = wide_keys.reshape(-1, heads_dev, HD)
    wide_values = wide_values.reshape(-1, heads_dev, HD)
    scale = 1.0 / math.sqrt(HD)
    span = WINDOW + block_rows
    query_pos = jnp.arange(block_rows, dtype=jnp.int32)[:, None]
    key_pos = jnp.arange(span, dtype=jnp.int32)[None, :]
    band = (key_pos > query_pos) & (key_pos <= query_pos + WINDOW)
    rows_q = queries.reshape(block_rows, heads_dev, HD)
    anchor = seq_index * length_dev + 0 - WINDOW
    valid = band & (anchor + key_pos >= 0)
    scores = (
        jnp.einsum("qhd,khd->hqk", rows_q, wide_keys, preferred_element_type=jnp.float32) * scale
    )
    scores = jnp.where(valid[None], scores, -1e30)
    top = jnp.max(scores, axis=-1, keepdims=True)
    expo = jnp.where(valid[None], jnp.exp(scores - top), 0.0)
    total = jnp.sum(expo, axis=-1)
    weights = expo.astype(jnp.bfloat16)
    summed = jnp.einsum("hqk,khe->qhe", weights, wide_values, preferred_element_type=jnp.float32)
    pieces = summed / jnp.transpose(total)[:, :, None]
    mixed = (normed + pieces).astype(jnp.bfloat16).reshape(length_dev, width)
    head_count = lax.axis_size("head")
    share = length_dev // head_count
    grouped = mixed.reshape(head_count, share, width)
    return jnp.dot(
        lax.all_to_all(grouped, "head", split_axis=0, concat_axis=2, tiled=True)[0],
        w_out,
        preferred_element_type=jnp.float32,
    ).astype(jnp.bfloat16)


def solution(mesh):
    return jax.shard_map(
        per_device,
        mesh=mesh,
        in_specs=(
            P(("groups", "seq"), "head"),
            P(("groups", "seq"), "head"),
            P(("groups", "seq"), "head"),
            P(),
        ),
        out_specs=P(("groups", "seq", "head"), None),
        check_vma=False,
    )
```
